32 devices in a mesh: recon: 1, slab: 32 (over z, y, x, core), coil: 1.
Axes of the slice: x: 2, y: 2, z: 4, core: 2. Of those that a mesh axis runs over, the one named last changes fastest.
Arguments:
- image: float32 [2, 192, 192, 192], P('recon', 'slab'), may hold values from -6 to 6
- prox_point: float32 [2, 192, 192, 192], P('recon', 'slab'), may hold values from -6 to 6
- dual: float32 [2, 192, 192, 192], P('recon', 'slab'), may hold values from -6 to 6
- adjoint_data: float32 [2, 192, 192, 192], P('recon', 'slab'), may hold values from -6 to 6
- coil_maps: float32 [1, 2, 192, 192, 192], P('coil', 'recon', 'slab'), may hold values from -4 to 4
- kernel: float32 [384, 384, 384], P('slab'), may hold values from 0.05 to 5
Outputs:
- image_new: float32 [2, 192, 192, 192], P('recon', 'slab')
- prox_new: float32 [2, 192, 192, 192], P('recon', 'slab')
- dual_new: float32 [2, 192, 192, 192], P('recon', 'slab')
The draws below stay inside these ranges and needn't reach their ends.
All inputs are finite; a program needn't handle non-finite values.
Results may differ from the reference program's by a relative error of at most 0.00015.
Values sent between devices are 32-bit elements; how exact they have to be, the bound alone decides.
A program may use at most 192 MiB of HBM per device.

```python
import math
import jax
import jax.numpy as jnp

IMG = 192
GRID = 384
COILS = 1


def steps_of(stream_key, dims, shards, smallest, top_value):
    def one(dim, parts):
        steps = jax.random.uniform(jax.random.fold_in(jax.random.fold_in(stream_key, 6), dim), (parts,), jnp.float32, smallest / len(shards), top_value / len(shards))
        return jnp.repeat(jnp.exp(steps), dims[dim] // parts).reshape((-1,) + (1,) * (len(dims) - dim - 1))

    gain = one(*shards[0])
    for cut in shards[1:]:
        gain = gain * one(*cut)
    return gain


def noise(stream_key, dims, spread, reach, shards=(), kind=jnp.bfloat16):
    gain = steps_of(stream_key, dims, shards, -0.22, 0.18) if shards else 1.0
    array = jax.random.normal(stream_key, dims, jnp.float32) * spread * gain
    return jnp.minimum(jnp.maximum(array, -reach), reach).astype(kind)


def setup_inputs(seed: int = 0, part: int = 0) -> dict:
    arg_keys = jax.random.split(jax.random.key(seed), 7)
    part_splits = jax.random.split(jax.random.fold_in(arg_keys[6], part), 7)
    image = noise(part_splits[0], (2, IMG, IMG, IMG), 1.0, 6.0, ((1, 32),), jnp.float32)
    prox_point = noise(part_splits[1], (2, IMG, IMG, IMG), 1.0, 6.0, ((1, 32),), jnp.float32)
    dual = noise(part_splits[2], (2, IMG, IMG, IMG), 0.5, 6.0, ((1, 32),), jnp.float32)
    adjoint_data = noise(part_splits[3], (2, IMG, IMG, IMG), 1.0, 6.0, ((1, 32),), jnp.float32)
    coil_maps = noise(part_splits[4], (COILS, 2, IMG, IMG, IMG), (2 * COILS) ** -0.5, 4.0, ((2, 32),), jnp.float32)
    kernel = jnp.clip(jnp.exp(math.log(5.0) - 4.6051702 * jax.random.uniform(arg_keys[5], (GRID, GRID, GRID), jnp.float32) ** steps_of(arg_keys[5], (GRID, GRID, GRID), ((0, 32),), -0.2, 0.2)), 0.05, 5.0)
    return dict(image=image, prox_point=prox_point, dual=dual, adjoint_data=adjoint_data, coil_maps=coil_maps, kernel=kernel)


half_root = 0.7071067811865476
shrink = 0.5
step_size = 0.25
penalty = 1.0

def pair_axis(values, axis_dim, offset):
    length = values.shape[axis_dim]
    layout = [1] * values.ndim
    layout[axis_dim] = length
    is_first = ((jnp.arange(length) - offset) % 2 == 0).reshape(layout)
    after_one = jnp.roll(values, -1, axis_dim)
    before_one = jnp.roll(values, 1, axis_dim)
    return jnp.where(is_first, (values + after_one) * half_root, (before_one - values) * half_root)

def first_mask(length, offset):
    return (jnp.arange(length) - offset) % 2 == 0

def spin(field, offset):
    coefs = field
    for axis_dim in (1, 2, 3):
        coefs = pair_axis(coefs, axis_dim, offset)
    keep = first_mask(field.shape[1], offset)[:, None, None] & first_mask(field.shape[2], offset)[None, :, None] & first_mask(field.shape[3], offset)[None, None, :]
    magnitude = jnp.sqrt(coefs[0] * coefs[0] + coefs[1] * coefs[1])
    factor = jnp.maximum(magnitude - shrink, 0.0) / jnp.maximum(magnitude, shrink)
    coefs = jnp.where(keep[None], coefs, coefs * factor[None])
    for axis_dim in (3, 2, 1):
        coefs = pair_axis(coefs, axis_dim, offset)
    return coefs

def reference(image, prox_point, dual, adjoint_data, coil_maps, kernel):
    picture = image[0] + 1j * image[1]
    spectrum_gain = jnp.transpose(kernel, (2, 0, 1))
    normal = jnp.zeros(picture.shape, picture.dtype)
    for coil_index in range(COILS):
        profile = coil_maps[coil_index, 0] + 1j * coil_maps[coil_index, 1]
        padded = jnp.pad(profile * picture, ((0, GRID - IMG), (0, GRID - IMG), (0, GRID - IMG)))
        filtered = jnp.fft.ifftn(jnp.fft.fftn(padded) * spectrum_gain)[:IMG, :IMG, :IMG]
        normal = normal + jnp.conj(profile) * filtered
    normal_parts = jnp.stack([jnp.real(normal), jnp.imag(normal)]).astype(image.dtype)
    image_new = image - step_size * (normal_parts - adjoint_data + penalty * (image - prox_point + dual))
    merged = image_new + dual
    prox_new = 0.5 * (spin(merged, 0) + spin(merged, 1))
    dual_new = dual + image_new - prox_new
    return (image_new, prox_new, dual_new)
```

```python
import functools
import math

import jax
import jax.numpy as jnp
import numpy as np
from jax import lax
from jax.experimental import pallas as pl
from jax.experimental.pallas import tpu as pltpu
from jax.sharding import PartitionSpec as P

half_root = 0.7071067811865476
shrink = 0.5
step_size = 0.25
penalty = 1.0
MESH = pl.DeviceIdType.MESH
f32 = jnp.float32
bf16 = jnp.bfloat16
LANES = 128


def halves(table):
    table = table.astype(np.float32)
    hi = table.astype(bf16)
    lo = (table - hi.astype(np.float32)).astype(bf16)
    return np.stack([hi, lo])


def tables_of(grid_len, width, n, chunks, group, dense):
    cells = np.arange(width)
    freqs = np.arange(grid_len)
    angle = 2.0 * math.pi / grid_len * (np.outer(cells, freqs) % grid_len)
    cos, sin = np.cos(angle), np.sin(angle)
    table_x = np.block([[cos, -sin], [sin, cos]])
    table_z = np.concatenate([cos.T, sin.T])
    table_iz = np.concatenate([cos, sin]) / grid_len
    if not dense:
        by_plane = np.arange(width).reshape(n, -1).T.reshape(-1)
        table_z = table_z[:, by_plane]
        table_iz = np.concatenate([cos[by_plane], sin[by_plane]]) / grid_len
    table_ix = np.block([[cos.T, sin.T], [-sin.T, cos.T]]) / grid_len
    own = chunks * group
    c, j, d = np.meshgrid(np.arange(chunks), np.arange(group), np.arange(n), indexing="ij")
    order = (d * own + c * group + j).reshape(chunks, group * n)
    table_y = np.concatenate([cos.T[order], sin.T[order]], axis=1)
    j, c, s = np.meshgrid(np.arange(group), np.arange(chunks), np.arange(n), indexing="ij")
    order = (s * own + c * group + j).reshape(-1)
    table_iy = np.concatenate([cos[:, order], sin[:, order]]) / grid_len
    return [halves(t) for t in (table_y, table_x, table_z, table_iz, table_ix, table_iy)]


def split(values):
    hi = values.astype(bf16)
    return hi, (values - hi.astype(f32)).astype(bf16)


def mm(a, b):
    return jnp.dot(a, b, preferred_element_type=f32)


def right(values, table):
    hi, lo = split(values)
    return mm(hi, table[0]) + mm(lo, table[0]) + mm(hi, table[1])


def left(table_hi, table_lo, values):
    hi, lo = split(values)
    return mm(table_hi, hi) + mm(table_hi, lo) + mm(table_lo, hi)


def turned(values, sign):
    half = values.shape[-1] // 2
    low, high = values[:, :half], values[:, half:]
    return jnp.concatenate([high * sign, low * -sign], axis=1)


def take(ref, rows):
    return jnp.concatenate([ref[l, rows, :] for l in range(ref.shape[0])], axis=1)


def put(ref, rows, values):
    for l in range(ref.shape[0]):
        ref[l, rows, :] = values[:, l * LANES : (l + 1) * LANES]


def filter_kernel(
    n, planes, chunks, group,
    field, gain_in, ty, tx, tz, tiz, tix, tiy, out,
    send, recv, back, home, gain, wide,
    send_sem, recv_sem, back_sem, home_sem, gain_sem,
):
    me = lax.axis_index("slab")
    width = field.shape[1]
    rows = send.shape[1] // (n * chunks)
    total = n * rows
    if rows == planes * group:
        spans = [(0, n * planes, group)]
    else:
        spans = [(z * group, n, rows) for z in range(planes)]

    gain_copy = pltpu.make_async_copy(gain_in, gain, gain_sem)
    gain_copy.start()
    barrier = pltpu.get_barrier_semaphore()

    def greet(i, carry):
        pl.semaphore_signal(
            barrier, inc=1, device_id={"slab": lax.rem(me + i, n)}, device_id_type=MESH
        )
        return carry

    lax.fori_loop(1, n, greet, 0)

    def push(c, source, target, s_sem, r_sem):
        def one(i, carry):
            to = lax.rem(me + i, n)
            pltpu.make_async_remote_copy(
                src_ref=source.at[:, pl.ds(pl.multiple_of(c * total + to * rows, 8), rows)],
                dst_ref=target.at[:, pl.ds(pl.multiple_of(c * total + me * rows, 8), rows)],
                send_sem=s_sem.at[c],
                recv_sem=r_sem.at[c],
                device_id={"slab": to},
                device_id_type=MESH,
            ).start()
            return carry

        lax.fori_loop(1, n, one, 0)
        own = pl.ds(pl.multiple_of(c * total + me * rows, 8), rows)
        pltpu.make_async_copy(source.at[:, own], target.at[:, own], r_sem.at[c]).start()

    def arrived(c, target, r_sem):
        span = target.at[:, pl.ds(pl.multiple_of(c * total, 8), total)]
        pltpu.make_async_copy(span, span, r_sem.at[c]).wait()

    def left_sent(c, source, s_sem):
        span = source.at[:, pl.ds(pl.multiple_of(c * total, 8), total - rows)]
        pltpu.make_async_copy(span, span, s_sem.at[c]).wait()

    def forward_y(c):
        def plane(z, carry):
            both = left(ty[0, c], ty[1, c], field[z])
            half = group * n
            lines_y = both[:half] + turned(both[half:], 1.0)
            for j in range(group):
                at = pl.ds(c * total + z * group + j, n, stride=rows)
                put(send, at, lines_y[j * n : (j + 1) * n])
            return carry

        lax.fori_loop(0, planes, plane, 0)

    for c in range(chunks):
        forward_y(c)
        if c == 0:
            pl.semaphore_wait(barrier, n - 1)
        push(c, send, recv, send_sem, recv_sem)

    gain_copy.wait()

    def flip(k, carry):
        gain[k] = jnp.transpose(gain[k])
        return carry

    lax.fori_loop(0, chunks * group, flip, 0)

    block = total // 2

    def middle(c, carry):
        arrived(c, recv, recv_sem)

        def forward_x(b, inner):
            at = pl.multiple_of(b * block, 8)
            start = pl.multiple_of(c * total + b * block, 8)
            put(wide, pl.ds(at, block), right(take(recv, pl.ds(start, block)), tx))
            return inner

        lax.fori_loop(0, 2, forward_x, 0)

        def plane(j, inner):
            lines_x = jnp.concatenate(
                [take(wide, pl.ds(j + at, size, stride=step)) for at, size, step in spans], axis=0
            )
            both = left(tz[0], tz[1], lines_x)
            half = both.shape[0] // 2
            spectrum = both[:half] + turned(both[half:], 1.0)
            factor = gain[c * group + j]
            spectrum = spectrum * jnp.concatenate([factor, factor], axis=1)
            both = left(tiz[0], tiz[1], spectrum)
            half = both.shape[0] // 2
            lines_z = both[:half] + turned(both[half:], -1.0)
            for k, (at, size, step) in enumerate(spans):
                put(wide, pl.ds(j + at, size, stride=step), lines_z[k * size : (k + 1) * size])
            return inner

        lax.fori_loop(0, group, plane, 0)

        def inverse_x(b, inner):
            at = pl.multiple_of(b * block, 8)
            start = pl.multiple_of(c * total + b * block, 8)
            put(back, pl.ds(start, block), right(take(wide, pl.ds(at, block)), tix))
            return inner

        lax.fori_loop(0, 2, inverse_x, 0)
        push(c, back, home, back_sem, home_sem)
        return carry

    lax.fori_loop(0, chunks, middle, 0)
    for c in range(chunks):
        arrived(c, home, home_sem)

    def inverse_y(z, carry):
        lines_y = jnp.concatenate(
            [
                take(home, pl.ds(z * group + j, n * chunks, stride=rows))
                for j in range(group)
            ],
            axis=0,
        )
        both = left(tiy[0], tiy[1], lines_y)
        half = both.shape[0] // 2
        out[z] = both[:half] + turned(both[half:], -1.0)
        return carry

    lax.fori_loop(0, planes, inverse_y, 0)
    for c in range(chunks):
        left_sent(c, send, send_sem)
        left_sent(c, back, back_sem)


def filtered(field, kernel, n):
    planes, width, double = field.shape
    own, grid_len, _ = kernel.shape
    fits = [g for g in range(1, own + 1) if own % g == 0 and g * planes % 8 == 0]
    group = fits[0] if fits else own
    chunks = own // group
    rows = -(-planes * group // 8) * 8
    total = n * rows
    tables = tables_of(grid_len, width, n, chunks, group, rows == planes * group)
    vmem = pl.BlockSpec(memory_space=pltpu.VMEM)
    flat = pltpu.VMEM((double // LANES, chunks * total, LANES), f32)
    dma = pltpu.SemaphoreType.DMA
    tables[0] = tables[0].reshape(2, chunks, 2 * group * n, width)
    return pl.pallas_call(
        functools.partial(filter_kernel, n, planes, chunks, group),
        out_shape=jax.ShapeDtypeStruct(field.shape, f32),
        in_specs=[vmem, pl.BlockSpec(memory_space=pl.ANY)] + [vmem] * 6,
        out_specs=vmem,
        scratch_shapes=[
            flat, flat, flat, flat,
            pltpu.VMEM(kernel.shape, f32),
            pltpu.VMEM((2 * grid_len // LANES, total, LANES), f32),
            dma((chunks,)), dma((chunks,)), dma((chunks,)), dma((chunks,)), dma(()),
        ],
        compiler_params=pltpu.CompilerParams(
            collective_id=0, has_side_effects=True, vmem_limit_bytes=60 * 1024 * 1024
        ),
        name="filtered",
    )(field, kernel, *tables)


def pair(values, axis, first):
    length = values.shape[axis]
    after_one = pltpu.roll(values, length - 1, axis)
    before_one = pltpu.roll(values, 1, axis)
    return jnp.where(first, values + after_one, before_one - values)


def blocks(first, second, offset):
    shape = first[0].shape
    row_first = (lax.broadcasted_iota(jnp.int32, shape, 0) + offset) % 2 == 0
    col_first = (lax.broadcasted_iota(jnp.int32, shape, 1) + offset) % 2 == 0
    norm = half_root * half_root * half_root
    sums = [a + b for a, b in zip(first, second)]
    diffs = [a - b for a, b in zip(first, second)]
    result = []
    for which, parts in ((0, sums), (1, diffs)):
        coefs = [pair(pair(p, 0, row_first), 1, col_first) * norm for p in parts]
        magnitude = jnp.sqrt(coefs[0] * coefs[0] + coefs[1] * coefs[1])
        factor = jnp.maximum(magnitude - shrink, 0.0) / jnp.maximum(magnitude, shrink)
        if which == 0:
            factor = jnp.where(row_first & col_first, 1.0, factor)
        result.append(
            [pair(pair(p * factor, 1, col_first), 0, row_first) * norm for p in coefs]
        )
    low = [a + b for a, b in zip(*result)]
    high = [a - b for a, b in zip(*result)]
    return low, high


def spin_kernel(merged, below, above, image_new, dual, prox, dual_new):
    planes = merged.shape[1]

    def read(z):
        return [merged[0, z], merged[1, z]]

    def even(k, carry):
        low, high = blocks(read(2 * k), read(2 * k + 1), 0)
        for part in range(2):
            prox[part, 2 * k] = 0.5 * low[part]
            prox[part, 2 * k + 1] = 0.5 * high[part]
        return carry

    lax.fori_loop(0, planes // 2, even, 0)

    def finish(part, z, value):
        full = prox[part, z] + 0.5 * value
        prox[part, z] = full
        dual_new[part, z] = dual[part, z] + image_new[part, z] - full

    def odd(k, carry):
        low, high = blocks(read(2 * k + 1), read(2 * k + 2), 1)
        for part in range(2):
            finish(part, 2 * k + 1, low[part])
            finish(part, 2 * k + 2, high[part])
        return carry

    lax.fori_loop(0, planes // 2 - 1, odd, 0)
    _, high = blocks([below[0, 0], below[1, 0]], read(0), 1)
    low, _ = blocks(read(planes - 1), [above[0, 0], above[1, 0]], 1)
    for part in range(2):
        finish(part, 0, high[part])
        finish(part, planes - 1, low[part])


def pair_local(values, axis_dim, offset):
    length = values.shape[axis_dim]
    layout = [1] * values.ndim
    layout[axis_dim] = length
    is_first = ((jnp.arange(length) - offset) % 2 == 0).reshape(layout)
    after_one = jnp.roll(values, -1, axis_dim)
    before_one = jnp.roll(values, 1, axis_dim)
    return jnp.where(is_first, (values + after_one) * half_root, (before_one - values) * half_root)


def pair_planes(extended, own_first):
    middle = extended[:, 1:-1]
    after_one = extended[:, 2:]
    before_one = extended[:, :-2]
    marked = own_first[None, :, None, None]
    return jnp.where(marked, (middle + after_one) * half_root, (before_one - middle) * half_root)


def spin(extended, base, offset):
    total_planes = extended.shape[1]
    global_plane = base - 1 + jnp.arange(total_planes, dtype=jnp.int32)
    plane_first = (global_plane - offset) % 2 == 0
    own_first = plane_first[1:-1]
    lower_rim = (extended[:, :1] + extended[:, 1:2]) * half_root
    upper_rim = (extended[:, -2:-1] - extended[:, -1:]) * half_root
    coefs = jnp.concatenate([lower_rim, pair_planes(extended, own_first), upper_rim], axis=1)
    coefs = pair_local(coefs, 2, offset)
    coefs = pair_local(coefs, 3, offset)
    rows_first = (jnp.arange(extended.shape[2]) - offset) % 2 == 0
    cols_first = (jnp.arange(extended.shape[3]) - offset) % 2 == 0
    keep = plane_first[:, None, None] & rows_first[None, :, None] & cols_first[None, None, :]
    magnitude = jnp.sqrt(coefs[0] * coefs[0] + coefs[1] * coefs[1])
    factor = jnp.maximum(magnitude - shrink, 0.0) / jnp.maximum(magnitude, shrink)
    coefs = jnp.where(keep[None], coefs, coefs * factor[None])
    coefs = pair_local(coefs, 3, offset)
    coefs = pair_local(coefs, 2, offset)
    return pair_planes(coefs, own_first)


def on_device(n, image, prox_point, dual, adjoint_data, coil_maps, kernel):
    width = image.shape[3]
    local_real = 0.0
    local_imag = 0.0
    for coil in range(coil_maps.shape[0]):
        sens_real = coil_maps[coil, 0]
        sens_imag = coil_maps[coil, 1]
        field = jnp.concatenate(
            [sens_real * image[0] - sens_imag * image[1], sens_real * image[1] + sens_imag * image[0]],
            axis=-1,
        )
        back = filtered(field, kernel, n)
        back_real, back_imag = back[..., :width], back[..., width:]
        local_real = local_real + (sens_real * back_real + sens_imag * back_imag)
        local_imag = local_imag + (sens_real * back_imag - sens_imag * back_real)
    normal_real, normal_imag = lax.psum((local_real, local_imag), "coil")
    normal = jnp.stack([normal_real, normal_imag])
    image_new = image - step_size * (normal - adjoint_data + penalty * (image - prox_point + dual))
    merged = image_new + dual
    planes = merged.shape[1]
    below = lax.ppermute(merged[:, -1:], "slab", [(i, (i + 1) % n) for i in range(n)])
    above = lax.ppermute(merged[:, :1], "slab", [((i + 1) % n, i) for i in range(n)])
    if planes % 2:
        extended = jnp.concatenate([below, merged, above], axis=1)
        base = lax.axis_index("slab") * planes
        prox_new = 0.5 * (spin(extended, base, 0) + spin(extended, base, 1))
        return (image_new, prox_new, dual + image_new - prox_new)
    vmem = pl.BlockSpec(memory_space=pltpu.VMEM)
    prox_new, dual_new = pl.pallas_call(
        spin_kernel,
        out_shape=[jax.ShapeDtypeStruct(image.shape, f32)] * 2,
        in_specs=[vmem] * 5,
        out_specs=[vmem] * 2,
        compiler_params=pltpu.CompilerParams(vmem_limit_bytes=48 * 1024 * 1024),
        name="spin",
    )(merged, below, above, image_new, dual)
    return (image_new, prox_new, dual_new)


def solution(mesh):
    n = mesh.shape["slab"]
    field = P("recon", "slab", None, None)
    return jax.shard_map(
        functools.partial(on_device, n),
        mesh=mesh,
        in_specs=(field, field, field, field, P("coil", "recon", "slab", None, None), P("slab", None, None)),
        out_specs=(field, field, field),
        check_vma=False,
    )
```

```python
import functools
import math

import jax
import jax.numpy as jnp
import numpy as np
from jax import lax
from jax.experimental import pallas as pl
from jax.experimental.pallas import tpu as pltpu
from jax.sharding import PartitionSpec as P

half_root = 0.7071067811865476
shrink = 0.5
step_size = 0.25
penalty = 1.0
MESH = pl.DeviceIdType.MESH
f32 = jnp.float32
bf16 = jnp.bfloat16
LANES = 128


def halves(table):
    table = table.astype(np.float32)
    hi = table.astype(bf16)
    lo = (table - hi.astype(np.float32)).astype(bf16)
    return np.stack([hi, lo])


def tables_of(grid_len, width, n, chunks, group, dense):
    cells = np.arange(width)
    freqs = np.arange(grid_len)
    angle = 2.0 * math.pi / grid_len * (np.outer(cells, freqs) % grid_len)
    cos, sin = np.cos(angle), np.sin(angle)
    table_x = np.block([[cos, -sin], [sin, cos]])
    table_z = np.concatenate([cos.T, sin.T])
    table_iz = np.concatenate([cos, sin]) / grid_len
    if not dense:
        by_plane = np.arange(width).reshape(n, -1).T.reshape(-1)
        table_z = table_z[:, by_plane]
        table_iz = np.concatenate([cos[by_plane], sin[by_plane]]) / grid_len
    table_ix = np.block([[cos.T, sin.T], [-sin.T, cos.T]]) / grid_len
    own = chunks * group
    c, j, d = np.meshgrid(np.arange(chunks), np.arange(group), np.arange(n), indexing="ij")
    order = (d * own + c * group + j).reshape(chunks, group * n)
    table_y = np.concatenate([cos.T[order], sin.T[order]], axis=1)
    j, c, s = np.meshgrid(np.arange(group), np.arange(chunks), np.arange(n), indexing="ij")
    order = (s * own + c * group + j).reshape(-1)
    table_iy = np.concatenate([cos[:, order], sin[:, order]]) / grid_len
    return [halves(t) for t in (table_y, table_x, table_z, table_iz, table_ix, table_iy)]


def split(values):
    hi = values.astype(bf16)
    return hi, (values - hi.astype(f32)).astype(bf16)


def mm(a, b):
    return jnp.dot(a, b, preferred_element_type=f32)


def right(values, table):
    hi, lo = split(values)
    return mm(hi, table[0]) + mm(lo, table[0]) + mm(hi, table[1])


def left(table_hi, table_lo, values):
    hi, lo = split(values)
    return mm(table_hi, hi) + mm(table_hi, lo) + mm(table_lo, hi)


def turned(values, sign):
    half = values.shape[-1] // 2
    low, high = values[:, :half], values[:, half:]
    return jnp.concatenate([high * sign, low * -sign], axis=1)


def take(ref, rows):
    return jnp.concatenate([ref[l, rows, :] for l in range(ref.shape[0])], axis=1)


def put(ref, rows, values):
    for l in range(ref.shape[0]):
        ref[l, rows, :] = values[:, l * LANES : (l + 1) * LANES]


def filter_kernel(n, planes, chunks, group, field, gain_in, ty, tx, tz, tiz, tix, tiy, out, *scratch):
    def finish(z, value):
        out[z] = value

    def inverse(plane):
        lax.fori_loop(0, planes, plane, 0)

    filter_body(
        n, planes, chunks, group, lambda z: field[z], finish, (lambda: None, lambda: None), inverse,
        gain_in, ty, tx, tz, tiz, tix, tiy, *scratch,
    )


def spin_pair(mg, px, table, edge, first, second, offset, add):
    count = edge // 2

    def rows(plane, odd):
        return pl.ds(plane * edge + odd, count, stride=2)

    def lines(plane):
        even, odd = take(mg, rows(plane, 0)), take(mg, rows(plane, 1))
        return (odd, pltpu.roll(even, count - 1, 0)) if offset else (even, odd)

    (f0, s0), (f1, s1) = lines(first), lines(second)
    uf, us, vf, vs = f0 + f1, s0 + s1, f0 - f1, s0 - s1
    cells = jnp.concatenate([uf + us, uf - us, vf + vs, vf - vs], axis=0)

    def along_x(values):
        hi, lo = split(values)
        return mm(hi, table[offset]) + mm(lo, table[offset])

    coefs = along_x(cells)
    squares = coefs * coefs
    half = squares.shape[1] // 2
    squares = squares + jnp.concatenate([squares[:, half:], squares[:, :half]], axis=1)
    factor = 1.0 - lax.rsqrt(jnp.maximum(0.5 * squares, 1.0))
    row = lax.broadcasted_iota(jnp.int32, factor.shape, 0)
    col = lax.broadcasted_iota(jnp.int32, factor.shape, 1)
    factor = jnp.where((row < count) & ((col + offset) % 2 == 0), 1.0, factor)
    cells = along_x(coefs * factor) * 0.0625
    uf, us, vf, vs = (cells[k * count : (k + 1) * count] for k in range(4))
    uf, us, vf, vs = uf + us, uf - us, vf + vs, vf - vs
    for plane, f, s in ((first, uf + vf, us + vs), (second, uf - vf, us - vs)):
        even, odd = (pltpu.roll(s, 1, 0), f) if offset else (f, s)
        if add:
            even = even + take(px, rows(plane, 0))
            odd = odd + take(px, rows(plane, 1))
        put(px, rows(plane, 0), even)
        put(px, rows(plane, 1), odd)


def step_kernel(
    n, planes, chunks, group,
    image, coil, late_a, late_b, late_c, gain_in, ty,
    ltx, ltz, ltiz, ltix, ltiy, lpx,
    image_new, prox_new, dual_new,
    prox_point, dual, adjoint, tx, tz, tiz, tix, tiy, table, mg, px,
    late_sem, halo_out, halo_in, *scratch,
):
    me = lax.axis_index("slab")
    edge, width = image.shape[2:]
    pairs = [
        (ltx, tx), (ltz, tz), (ltiz, tiz), (ltix, tix), (ltiy, tiy), (lpx, table),
        (late_a, prox_point), (late_b, dual), (late_c, adjoint),
    ]
    copies = [pltpu.make_async_copy(a, b, late_sem.at[k]) for k, (a, b) in enumerate(pairs)]

    def begin():
        for copy in copies:
            copy.start()

    def ready():
        for copy in copies:
            copy.wait()

    def field(z):
        sr, si, re, im = coil[0, z], coil[1, z], image[0, z], image[1, z]
        return jnp.concatenate([sr * re - si * im, sr * im + si * re], axis=1)

    def finish(z, value):
        back = (value[:, :width], value[:, width:])
        sr, si = coil[0, z], coil[1, z]
        normal = (sr * back[0] + si * back[1], sr * back[1] - si * back[0])
        merged = []
        for part in range(2):
            old, point, scaled = image[part, z], prox_point[part, z], dual[part, z]
            new = old - step_size * (normal[part] - adjoint[part, z] + penalty * (old - point + scaled))
            image_new[part, z] = new
            merged.append(new + scaled)
        put(mg, pl.ds((z + 1) * edge, edge), jnp.concatenate(merged, axis=1))

    def span(plane):
        return mg.at[:, pl.ds(plane * edge, edge)]

    up = pltpu.make_async_remote_copy(
        src_ref=span(planes), dst_ref=span(0), send_sem=halo_out.at[0], recv_sem=halo_in.at[0],
        device_id={"slab": lax.rem(me + 1, n)}, device_id_type=MESH,
    )
    down = pltpu.make_async_remote_copy(
        src_ref=span(1), dst_ref=span(planes + 1), send_sem=halo_out.at[1], recv_sem=halo_in.at[1],
        device_id={"slab": lax.rem(me + n - 1, n)}, device_id_type=MESH,
    )

    def inverse(plane):
        def rim(k, carry):
            return plane(k * (planes - 1), carry)

        lax.fori_loop(0, 2, rim, 0)
        up.start()
        down.start()
        lax.fori_loop(1, planes - 1, plane, 0)

    filter_body(
        n, planes, chunks, group, field, finish, (begin, ready), inverse,
        gain_in, ty, tx, tz, tiz, tix, tiy, *scratch,
    )

    for plane in (0, planes + 1):
        put(px, pl.ds(plane * edge, edge), jnp.zeros((edge, 2 * width), f32))

    def even(k, carry):
        spin_pair(mg, px, table, edge, 2 * k + 1, 2 * k + 2, 0, False)
        return carry

    def odd(k, carry):
        spin_pair(mg, px, table, edge, 2 * k, 2 * k + 1, 1, True)
        return carry

    def rim(k, carry):
        return odd(k * (planes // 2), carry)

    def close(z, carry):
        at = pl.ds((z + 1) * edge, edge)
        prox = take(px, at)
        scaled = take(mg, at) - prox
        for part in range(2):
            prox_new[part, z] = prox[:, part * width : (part + 1) * width]
            dual_new[part, z] = scaled[:, part * width : (part + 1) * width]
        return carry

    lax.fori_loop(0, planes // 2, even, 0)
    lax.fori_loop(1, planes // 2, odd, 0)
    lax.fori_loop(1, planes - 1, close, 0)
    up.wait()
    down.wait()
    lax.fori_loop(0, 2, rim, 0)
    lax.fori_loop(0, 2, lambda k, carry: close(k * (planes - 1), carry), 0)


def filter_body(
    n, planes, chunks, group, field, finish, late, inverse,
    gain_in, ty, tx, tz, tiz, tix, tiy,
    send, recv, back, home, gain, wide,
    send_sem, recv_sem, back_sem, home_sem, gain_sem,
):
    begin, ready = late
    me = lax.axis_index("slab")
    rows = send.shape[1] // (n * chunks)
    total = n * rows
    if rows == planes * group:
        spans = [(0, n * planes, group)]
    else:
        spans = [(z * group, n, rows) for z in range(planes)]

    gain_copy = pltpu.make_async_copy(gain_in, gain, gain_sem)
    gain_copy.start()
    barrier = pltpu.get_barrier_semaphore()

    def greet(i, carry):
        pl.semaphore_signal(
            barrier, inc=1, device_id={"slab": lax.rem(me + i, n)}, device_id_type=MESH
        )
        return carry

    lax.fori_loop(1, n, greet, 0)
    begin()

    def push(c, source, target, s_sem, r_sem):
        def one(i, carry):
            to = lax.rem(me + i, n)
            pltpu.make_async_remote_copy(
                src_ref=source.at[:, pl.ds(pl.multiple_of(c * total + to * rows, 8), rows)],
                dst_ref=target.at[:, pl.ds(pl.multiple_of(c * total + me * rows, 8), rows)],
                send_sem=s_sem.at[c],
                recv_sem=r_sem.at[c],
                device_id={"slab": to},
                device_id_type=MESH,
            ).start()
            return carry

        lax.fori_loop(1, n, one, 0)
        own = pl.ds(pl.multiple_of(c * total + me * rows, 8), rows)
        pltpu.make_async_copy(source.at[:, own], target.at[:, own], r_sem.at[c]).start()

    def arrived(c, target, r_sem):
        span = target.at[:, pl.ds(pl.multiple_of(c * total, 8), total)]
        pltpu.make_async_copy(span, span, r_sem.at[c]).wait()

    def left_sent(c, source, s_sem):
        span = source.at[:, pl.ds(pl.multiple_of(c * total, 8), total - rows)]
        pltpu.make_async_copy(span, span, s_sem.at[c]).wait()

    def forward_y(c):
        def plane(z, carry):
            both = left(ty[0, c], ty[1, c], field(z))
            half = group * n
            lines_y = both[:half] + turned(both[half:], 1.0)
            for j in range(group):
                at = pl.ds(c * total + z * group + j, n, stride=rows)
                put(send, at, lines_y[j * n : (j + 1) * n])
            return carry

        lax.fori_loop(0, planes, plane, 0)

    for c in range(chunks):
        forward_y(c)
        if c == 0:
            pl.semaphore_wait(barrier, n - 1)
        push(c, send, recv, send_sem, recv_sem)

    gain_copy.wait()
    ready()

    def flip(k, carry):
        gain[k] = jnp.transpose(gain[k])
        return carry

    lax.fori_loop(0, chunks * group, flip, 0)

    block = total // 2

    def middle(c, carry):
        arrived(c, recv, recv_sem)

        def forward_x(b, inner):
            at = pl.multiple_of(b * block, 8)
            start = pl.multiple_of(c * total + b * block, 8)
            put(wide, pl.ds(at, block), right(take(recv, pl.ds(start, block)), tx))
            return inner

        lax.fori_loop(0, 2, forward_x, 0)

        def plane(j, inner):
            lines_x = jnp.concatenate(
                [take(wide, pl.ds(j + at, size, stride=step)) for at, size, step in spans], axis=0
            )
            both = left(tz[0], tz[1], lines_x)
            half = both.shape[0] // 2
            spectrum = both[:half] + turned(both[half:], 1.0)
            factor = gain[c * group + j]
            spectrum = spectrum * jnp.concatenate([factor, factor], axis=1)
            both = left(tiz[0], tiz[1], spectrum)
            half = both.shape[0] // 2
            lines_z = both[:half] + turned(both[half:], -1.0)
            for k, (at, size, step) in enumerate(spans):
                put(wide, pl.ds(j + at, size, stride=step), lines_z[k * size : (k + 1) * size])
            return inner

        lax.fori_loop(0, group, plane, 0)

        def inverse_x(b, inner):
            at = pl.multiple_of(b * block, 8)
            start = pl.multiple_of(c * total + b * block, 8)
            put(back, pl.ds(start, block), right(take(wide, pl.ds(at, block)), tix))
            return inner

        lax.fori_loop(0, 2, inverse_x, 0)
        push(c, back, home, back_sem, home_sem)
        return carry

    lax.fori_loop(0, chunks, middle, 0)
    for c in range(chunks):
        arrived(c, home, home_sem)

    def inverse_y(z, carry):
        lines_y = jnp.concatenate(
            [
                take(home, pl.ds(z * group + j, n * chunks, stride=rows))
                for j in range(group)
            ],
            axis=0,
        )
        both = left(tiy[0], tiy[1], lines_y)
        half = both.shape[0] // 2
        finish(z, both[:half] + turned(both[half:], -1.0))
        return carry

    inverse(inverse_y)
    for c in range(chunks):
        left_sent(c, send, send_sem)
        left_sent(c, back, back_sem)


def plan(shape, kernel, n):
    planes, width, double = shape
    own, grid_len, _ = kernel.shape
    fits = [g for g in range(1, own + 1) if own % g == 0 and g * planes % 8 == 0]
    group = fits[0] if fits else own
    chunks = own // group
    rows = -(-planes * group // 8) * 8
    total = n * rows
    tables = tables_of(grid_len, width, n, chunks, group, rows == planes * group)
    flat = pltpu.VMEM((double // LANES, chunks * total, LANES), f32)
    dma = pltpu.SemaphoreType.DMA
    tables[0] = tables[0].reshape(2, chunks, 2 * group * n, width)
    scratch = [
        flat, flat, flat, flat,
        pltpu.VMEM(kernel.shape, f32),
        pltpu.VMEM((2 * grid_len // LANES, total, LANES), f32),
        dma((chunks,)), dma((chunks,)), dma((chunks,)), dma((chunks,)), dma(()),
    ]
    return chunks, group, tables, scratch


def fused(image, prox_point, dual, adjoint, coil, kernel, n):
    _, planes, edge, width = image.shape
    chunks, group, tables, scratch = plan((planes, edge, 2 * width), kernel, n)
    haar = np.zeros((2, 2 * width, 2 * width), np.float32)
    for offset in range(2):
        for part in range(2):
            first = (np.arange(width // 2) * 2 + offset) % width + part * width
            second = (np.arange(width // 2) * 2 + offset + 1) % width + part * width
            haar[offset, first, first] = haar[offset, first, second] = 1.0
            haar[offset, second, first] = 1.0
            haar[offset, second, second] = -1.0
    tables.append(haar.astype(bf16))
    vmem = pl.BlockSpec(memory_space=pltpu.VMEM)
    apart = pl.BlockSpec(memory_space=pl.ANY)
    held = [pltpu.VMEM(image.shape, f32)] * 3
    held += [pltpu.VMEM(t.shape, bf16) for t in tables[1:]]
    lines = pltpu.VMEM((2 * width // LANES, (planes + 2) * edge, LANES), f32)
    dma = pltpu.SemaphoreType.DMA
    return pl.pallas_call(
        functools.partial(step_kernel, n, planes, chunks, group),
        out_shape=[jax.ShapeDtypeStruct(image.shape, f32)] * 3,
        in_specs=[vmem, vmem] + [apart] * 4 + [vmem] + [apart] * 6,
        out_specs=[vmem] * 3,
        scratch_shapes=held + [lines, lines, dma((9,)), dma((2,)), dma((2,))] + scratch,
        compiler_params=pltpu.CompilerParams(
            collective_id=0, has_side_effects=True, vmem_limit_bytes=67043328
        ),
        name="fused",
    )(image, coil, prox_point, dual, adjoint, kernel, *tables)


def filtered(field, kernel, n):
    planes = field.shape[0]
    chunks, group, tables, scratch = plan(field.shape, kernel, n)
    vmem = pl.BlockSpec(memory_space=pltpu.VMEM)
    return pl.pallas_call(
        functools.partial(filter_kernel, n, planes, chunks, group),
        out_shape=jax.ShapeDtypeStruct(field.shape, f32),
        in_specs=[vmem, pl.BlockSpec(memory_space=pl.ANY)] + [vmem] * 6,
        out_specs=vmem,
        scratch_shapes=scratch,
        compiler_params=pltpu.CompilerParams(
            collective_id=0, has_side_effects=True, vmem_limit_bytes=60 * 1024 * 1024
        ),
        name="filtered",
    )(field, kernel, *tables)


def pair(values, axis, first):
    length = values.shape[axis]
    after_one = pltpu.roll(values, length - 1, axis)
    before_one = pltpu.roll(values, 1, axis)
    return jnp.where(first, values + after_one, before_one - values)


def blocks(first, second, offset):
    shape = first[0].shape
    row_first = (lax.broadcasted_iota(jnp.int32, shape, 0) + offset) % 2 == 0
    col_first = (lax.broadcasted_iota(jnp.int32, shape, 1) + offset) % 2 == 0
    norm = half_root * half_root * half_root
    sums = [a + b for a, b in zip(first, second)]
    diffs = [a - b for a, b in zip(first, second)]
    result = []
    for which, parts in ((0, sums), (1, diffs)):
        coefs = [pair(pair(p, 0, row_first), 1, col_first) * norm for p in parts]
        magnitude = jnp.sqrt(coefs[0] * coefs[0] + coefs[1] * coefs[1])
        factor = jnp.maximum(magnitude - shrink, 0.0) / jnp.maximum(magnitude, shrink)
        if which == 0:
            factor = jnp.where(row_first & col_first, 1.0, factor)
        result.append(
            [pair(pair(p * factor, 1, col_first), 0, row_first) * norm for p in coefs]
        )
    low = [a + b for a, b in zip(*result)]
    high = [a - b for a, b in zip(*result)]
    return low, high


def spin_kernel(merged, below, above, image_new, dual, prox, dual_new):
    planes = merged.shape[1]

    def read(z):
        return [merged[0, z], merged[1, z]]

    def even(k, carry):
        low, high = blocks(read(2 * k), read(2 * k + 1), 0)
        for part in range(2):
            prox[part, 2 * k] = 0.5 * low[part]
            prox[part, 2 * k + 1] = 0.5 * high[part]
        return carry

    lax.fori_loop(0, planes // 2, even, 0)

    def finish(part, z, value):
        full = prox[part, z] + 0.5 * value
        prox[part, z] = full
        dual_new[part, z] = dual[part, z] + image_new[part, z] - full

    def odd(k, carry):
        low, high = blocks(read(2 * k + 1), read(2 * k + 2), 1)
        for part in range(2):
            finish(part, 2 * k + 1, low[part])
            finish(part, 2 * k + 2, high[part])
        return carry

    lax.fori_loop(0, planes // 2 - 1, odd, 0)
    _, high = blocks([below[0, 0], below[1, 0]], read(0), 1)
    low, _ = blocks(read(planes - 1), [above[0, 0], above[1, 0]], 1)
    for part in range(2):
        finish(part, 0, high[part])
        finish(part, planes - 1, low[part])


def pair_local(values, axis_dim, offset):
    length = values.shape[axis_dim]
    layout = [1] * values.ndim
    layout[axis_dim] = length
    is_first = ((jnp.arange(length) - offset) % 2 == 0).reshape(layout)
    after_one = jnp.roll(values, -1, axis_dim)
    before_one = jnp.roll(values, 1, axis_dim)
    return jnp.where(is_first, (values + after_one) * half_root, (before_one - values) * half_root)


def pair_planes(extended, own_first):
    middle = extended[:, 1:-1]
    after_one = extended[:, 2:]
    before_one = extended[:, :-2]
    marked = own_first[None, :, None, None]
    return jnp.where(marked, (middle + after_one) * half_root, (before_one - middle) * half_root)


def spin(extended, base, offset):
    total_planes = extended.shape[1]
    global_plane = base - 1 + jnp.arange(total_planes, dtype=jnp.int32)
    plane_first = (global_plane - offset) % 2 == 0
    own_first = plane_first[1:-1]
    lower_rim = (extended[:, :1] + extended[:, 1:2]) * half_root
    upper_rim = (extended[:, -2:-1] - extended[:, -1:]) * half_root
    coefs = jnp.concatenate([lower_rim, pair_planes(extended, own_first), upper_rim], axis=1)
    coefs = pair_local(coefs, 2, offset)
    coefs = pair_local(coefs, 3, offset)
    rows_first = (jnp.arange(extended.shape[2]) - offset) % 2 == 0
    cols_first = (jnp.arange(extended.shape[3]) - offset) % 2 == 0
    keep = plane_first[:, None, None] & rows_first[None, :, None] & cols_first[None, None, :]
    magnitude = jnp.sqrt(coefs[0] * coefs[0] + coefs[1] * coefs[1])
    factor = jnp.maximum(magnitude - shrink, 0.0) / jnp.maximum(magnitude, shrink)
    coefs = jnp.where(keep[None], coefs, coefs * factor[None])
    coefs = pair_local(coefs, 3, offset)
    coefs = pair_local(coefs, 2, offset)
    return pair_planes(coefs, own_first)


def on_device(n, coils, image, prox_point, dual, adjoint_data, coil_maps, kernel):
    width = image.shape[3]
    if coils == 1 and coil_maps.shape[0] == 1 and image.shape[1] % 2 == 0:
        return tuple(fused(image, prox_point, dual, adjoint_data, coil_maps[0], kernel, n))
    local_real = 0.0
    local_imag = 0.0
    for coil in range(coil_maps.shape[0]):
        sens_real = coil_maps[coil, 0]
        sens_imag = coil_maps[coil, 1]
        field = jnp.concatenate(
            [sens_real * image[0] - sens_imag * image[1], sens_real * image[1] + sens_imag * image[0]],
            axis=-1,
        )
        back = filtered(field, kernel, n)
        back_real, back_imag = back[..., :width], back[..., width:]
        local_real = local_real + (sens_real * back_real + sens_imag * back_imag)
        local_imag = local_imag + (sens_real * back_imag - sens_imag * back_real)
    normal_real, normal_imag = lax.psum((local_real, local_imag), "coil")
    normal = jnp.stack([normal_real, normal_imag])
    image_new = image - step_size * (normal - adjoint_data + penalty * (image - prox_point + dual))
    merged = image_new + dual
    planes = merged.shape[1]
    below = lax.ppermute(merged[:, -1:], "slab", [(i, (i + 1) % n) for i in range(n)])
    above = lax.ppermute(merged[:, :1], "slab", [((i + 1) % n, i) for i in range(n)])
    if planes % 2:
        extended = jnp.concatenate([below, merged, above], axis=1)
        base = lax.axis_index("slab") * planes
        prox_new = 0.5 * (spin(extended, base, 0) + spin(extended, base, 1))
        return (image_new, prox_new, dual + image_new - prox_new)
    vmem = pl.BlockSpec(memory_space=pltpu.VMEM)
    prox_new, dual_new = pl.pallas_call(
        spin_kernel,
        out_shape=[jax.ShapeDtypeStruct(image.shape, f32)] * 2,
        in_specs=[vmem] * 5,
        out_specs=[vmem] * 2,
        compiler_params=pltpu.CompilerParams(vmem_limit_bytes=48 * 1024 * 1024),
        name="spin",
    )(merged, below, above, image_new, dual)
    return (image_new, prox_new, dual_new)


def solution(mesh):
    n = mesh.shape["slab"]
    field = P("recon", "slab", None, None)
    return jax.shard_map(
        functools.partial(on_device, n, mesh.shape["coil"]),
        mesh=mesh,
        in_specs=(field, field, field, field, P("coil", "recon", "slab", None, None), P("slab", None, None)),
        out_specs=(field, field, field),
        check_vma=False,
    )
```

```python
import functools
import math

import jax
import jax.numpy as jnp
import numpy as np
from jax import lax
from jax.experimental import pallas as pl
from jax.experimental.pallas import tpu as pltpu
from jax.sharding import PartitionSpec as P

half_root = 0.7071067811865476
shrink = 0.5
step_size = 0.25
penalty = 1.0
MESH = pl.DeviceIdType.MESH
f32 = jnp.float32
bf16 = jnp.bfloat16
LANES = 128


def halves(table):
    table = table.astype(np.float32)
    hi = table.astype(bf16)
    lo = (table - hi.astype(np.float32)).astype(bf16)
    return np.stack([hi, lo])


def tables_of(grid_len, width, n, chunks, group, dense):
    cells = np.arange(width)
    freqs = np.arange(grid_len)
    angle = 2.0 * math.pi / grid_len * (np.outer(cells, freqs) % grid_len)
    cos, sin = np.cos(angle), np.sin(angle)
    table_x = np.block([[cos, -sin], [sin, cos]])
    table_z = np.concatenate([cos.T, sin.T])
    table_iz = np.concatenate([cos, sin]) / grid_len
    if not dense:
        by_plane = np.arange(width).reshape(n, -1).T.reshape(-1)
        table_z = table_z[:, by_plane]
        table_iz = np.concatenate([cos[by_plane], sin[by_plane]]) / grid_len
    table_ix = np.block([[cos.T, sin.T], [-sin.T, cos.T]]) / grid_len
    own = chunks * group
    c, j, d = np.meshgrid(np.arange(chunks), np.arange(group), np.arange(n), indexing="ij")
    order = (d * own + c * group + j).reshape(chunks, group * n)
    table_y = np.concatenate([cos.T[order], sin.T[order]], axis=1)
    c, j, s = np.meshgrid(np.arange(chunks), np.arange(group), np.arange(n), indexing="ij")
    order = (s * own + c * group + j).reshape(chunks, 1, -1)
    both = np.concatenate([cos, sin])[:, :] / grid_len
    table_iy = np.stack([both[:, order[c, 0]] for c in range(chunks)])
    return [halves(t) for t in (table_y, table_x, table_z, table_iz, table_ix, table_iy)]


def split(values):
    hi = values.astype(bf16)
    return hi, (values - hi.astype(f32)).astype(bf16)


def mm(a, b):
    return jnp.dot(a, b, preferred_element_type=f32)


def right(values, table):
    hi, lo = split(values)
    return mm(hi, table[0]) + mm(lo, table[0]) + mm(hi, table[1])


def left(table_hi, table_lo, values):
    hi, lo = split(values)
    return mm(table_hi, hi) + mm(table_hi, lo) + mm(table_lo, hi)


def turned(values, sign):
    half = values.shape[-1] // 2
    low, high = values[:, :half], values[:, half:]
    return jnp.concatenate([high * sign, low * -sign], axis=1)


def take(ref, rows):
    return jnp.concatenate([ref[l, rows, :] for l in range(ref.shape[0])], axis=1)


def put(ref, rows, values):
    for l in range(ref.shape[0]):
        ref[l, rows, :] = values[:, l * LANES : (l + 1) * LANES]


def filter_kernel(n, planes, chunks, group, field, gain_in, ty, tx, tz, tiz, tix, tiy, out, *scratch):
    def finish(z, value):
        out[z] = value

    def inverse(plane):
        lax.fori_loop(0, planes, plane, 0)

    filter_body(
        n, planes, chunks, group, lambda z: field[z], finish, (lambda: None, lambda: None), inverse,
        gain_in, ty, tx, tz, tiz, tix, tiy, *scratch,
    )


def spin_pair(mg, px, table, edge, first, second, offset, add):
    count = edge // 2

    def rows(plane, odd):
        return pl.ds(plane * edge + odd, count, stride=2)

    def lines(plane):
        even, odd = take(mg, rows(plane, 0)), take(mg, rows(plane, 1))
        return (odd, pltpu.roll(even, count - 1, 0)) if offset else (even, odd)

    (f0, s0), (f1, s1) = lines(first), lines(second)
    uf, us, vf, vs = f0 + f1, s0 + s1, f0 - f1, s0 - s1
    cells = jnp.concatenate([uf + us, uf - us, vf + vs, vf - vs], axis=0)

    def along_x(values):
        hi, lo = split(values)
        return mm(hi, table[offset]) + mm(lo, table[offset])

    coefs = along_x(cells)
    squares = coefs * coefs
    half = squares.shape[1] // 2
    squares = squares + jnp.concatenate([squares[:, half:], squares[:, :half]], axis=1)
    factor = 1.0 - lax.rsqrt(jnp.maximum(0.5 * squares, 1.0))
    row = lax.broadcasted_iota(jnp.int32, factor.shape, 0)
    col = lax.broadcasted_iota(jnp.int32, factor.shape, 1)
    factor = jnp.where((row < count) & ((col + offset) % 2 == 0), 1.0, factor)
    cells = along_x(coefs * factor) * 0.0625
    uf, us, vf, vs = (cells[k * count : (k + 1) * count] for k in range(4))
    uf, us, vf, vs = uf + us, uf - us, vf + vs, vf - vs
    for plane, f, s in ((first, uf + vf, us + vs), (second, uf - vf, us - vs)):
        even, odd = (pltpu.roll(s, 1, 0), f) if offset else (f, s)
        if add:
            even = even + take(px, rows(plane, 0))
            odd = odd + take(px, rows(plane, 1))
        put(px, rows(plane, 0), even)
        put(px, rows(plane, 1), odd)


def step_kernel(
    n, planes, chunks, group,
    image, coil, late_a, late_b, late_c, gain_in, ty,
    ltx, ltz, ltiz, ltix, ltiy, lpx,
    image_out, prox_out, dual_out,
    image_new, prox_new, dual_new, prox_point, dual, adjoint, tx, tz, tiz, tix, tiy, table, mg, px,
    late_sem, halo_out, halo_in, out_sem, *scratch,
):
    me = lax.axis_index("slab")
    edge, width = image.shape[2:]
    pairs = [
        (ltx, tx), (ltz, tz), (ltiz, tiz), (ltix, tix), (ltiy, tiy), (lpx, table),
        (late_a, prox_point), (late_b, dual), (late_c, adjoint),
    ]
    copies = [pltpu.make_async_copy(a, b, late_sem.at[k]) for k, (a, b) in enumerate(pairs)]

    def begin():
        for copy in copies:
            copy.start()

    def ready():
        for copy in copies:
            copy.wait()

    def field(z):
        sr, si, re, im = coil[0, z], coil[1, z], image[0, z], image[1, z]
        return jnp.concatenate([sr * re - si * im, sr * im + si * re], axis=1)

    def finish(z, value):
        back = (value[:, :width], value[:, width:])
        sr, si = coil[0, z], coil[1, z]
        normal = (sr * back[0] + si * back[1], sr * back[1] - si * back[0])
        merged = []
        for part in range(2):
            old, point, scaled = image[part, z], prox_point[part, z], dual[part, z]
            new = old - step_size * (normal[part] - adjoint[part, z] + penalty * (old - point + scaled))
            image_new[part, z] = new
            merged.append(new + scaled)
        put(mg, pl.ds((z + 1) * edge, edge), jnp.concatenate(merged, axis=1))

    def span(plane):
        return mg.at[:, pl.ds(plane * edge, edge)]

    up = pltpu.make_async_remote_copy(
        src_ref=span(planes), dst_ref=span(0), send_sem=halo_out.at[0], recv_sem=halo_in.at[0],
        device_id={"slab": lax.rem(me + 1, n)}, device_id_type=MESH,
    )
    down = pltpu.make_async_remote_copy(
        src_ref=span(1), dst_ref=span(planes + 1), send_sem=halo_out.at[1], recv_sem=halo_in.at[1],
        device_id={"slab": lax.rem(me + n - 1, n)}, device_id_type=MESH,
    )

    def inverse(plane):
        def rim(k, carry):
            return plane(k * (planes - 1), carry)

        lax.fori_loop(0, 2, rim, 0)
        up.start()
        down.start()
        lax.fori_loop(1, planes - 1, plane, 0)

    filter_body(
        n, planes, chunks, group, field, finish, (begin, ready), inverse,
        gain_in, ty, tx, tz, tiz, tix, tiy, *scratch,
    )

    written = [pltpu.make_async_copy(image_new, image_out, out_sem.at[0])]
    written[0].start()

    def write(k, start, size):
        for buffer, whole in ((prox_new, prox_out), (dual_new, dual_out)):
            part = pl.ds(start, size)
            copy = pltpu.make_async_copy(buffer.at[:, part], whole.at[:, part], out_sem.at[k])
            copy.start()
            written.append(copy)
            k += 1

    for plane in (0, planes + 1):
        put(px, pl.ds(plane * edge, edge), jnp.zeros((edge, 2 * width), f32))

    def even(k, carry):
        spin_pair(mg, px, table, edge, 2 * k + 1, 2 * k + 2, 0, False)
        return carry

    def odd(k, carry):
        spin_pair(mg, px, table, edge, 2 * k, 2 * k + 1, 1, True)
        return carry

    def rim(k, carry):
        return odd(k * (planes // 2), carry)

    def close(z, carry):
        at = pl.ds((z + 1) * edge, edge)
        prox = take(px, at)
        scaled = take(mg, at) - prox
        for part in range(2):
            prox_new[part, z] = prox[:, part * width : (part + 1) * width]
            dual_new[part, z] = scaled[:, part * width : (part + 1) * width]
        return carry

    lax.fori_loop(0, planes // 2, even, 0)
    lax.fori_loop(1, planes // 2, odd, 0)
    if planes > 2:
        lax.fori_loop(1, planes - 1, close, 0)
        write(1, 1, planes - 2)
    up.wait()
    down.wait()
    lax.fori_loop(0, 2, rim, 0)
    lax.fori_loop(0, 2, lambda k, carry: close(k * (planes - 1), carry), 0)
    write(3, 0, 1)
    write(5, planes - 1, 1)
    for copy in written:
        copy.wait()


def filter_body(
    n, planes, chunks, group, field, finish, late, inverse,
    gain_in, ty, tx, tz, tiz, tix, tiy,
    send, recv, back, home, gain, wide,
    send_sem, recv_sem, back_sem, home_sem, gain_sem,
):
    begin, ready = late
    me = lax.axis_index("slab")
    rows = send.shape[1] // (n * chunks)
    total = n * rows
    if rows == planes * group:
        spans = [(0, n * planes, group)]
    else:
        spans = [(z * group, n, rows) for z in range(planes)]

    gain_copy = pltpu.make_async_copy(gain_in, gain, gain_sem)
    gain_copy.start()
    barrier = pltpu.get_barrier_semaphore()

    def greet(i, carry):
        pl.semaphore_signal(
            barrier, inc=1, device_id={"slab": lax.rem(me + i, n)}, device_id_type=MESH
        )
        return carry

    lax.fori_loop(1, n, greet, 0)
    begin()

    def push(c, source, target, s_sem, r_sem):
        def one(i, carry):
            to = lax.rem(me + i, n)
            pltpu.make_async_remote_copy(
                src_ref=source.at[:, pl.ds(pl.multiple_of(c * total + to * rows, 8), rows)],
                dst_ref=target.at[:, pl.ds(pl.multiple_of(c * total + me * rows, 8), rows)],
                send_sem=s_sem.at[c],
                recv_sem=r_sem.at[c],
                device_id={"slab": to},
                device_id_type=MESH,
            ).start()
            return carry

        lax.fori_loop(1, n, one, 0)
        own = pl.ds(pl.multiple_of(c * total + me * rows, 8), rows)
        pltpu.make_async_copy(source.at[:, own], target.at[:, own], r_sem.at[c]).start()

    def arrived(c, target, r_sem):
        span = target.at[:, pl.ds(pl.multiple_of(c * total, 8), total)]
        pltpu.make_async_copy(span, span, r_sem.at[c]).wait()

    def left_sent(c, source, s_sem):
        span = source.at[:, pl.ds(pl.multiple_of(c * total, 8), total - rows)]
        pltpu.make_async_copy(span, span, s_sem.at[c]).wait()

    def forward_y(c):
        def plane(z, carry):
            both = left(ty[0, c], ty[1, c], field(z))
            half = group * n
            lines_y = both[:half] + turned(both[half:], 1.0)
            for j in range(group):
                at = pl.ds(c * total + z * group + j, n, stride=rows)
                put(send, at, lines_y[j * n : (j + 1) * n])
            return carry

        lax.fori_loop(0, planes, plane, 0)

    for c in range(chunks):
        forward_y(c)
        if c == 0:
            pl.semaphore_wait(barrier, n - 1)
        push(c, send, recv, send_sem, recv_sem)

    gain_copy.wait()
    ready()

    def flip(k, carry):
        gain[k] = jnp.transpose(gain[k])
        return carry

    lax.fori_loop(0, chunks * group, flip, 0)

    block = total // 2

    def middle(c, carry):
        arrived(c, recv, recv_sem)

        def forward_x(b, inner):
            at = pl.multiple_of(b * block, 8)
            start = pl.multiple_of(c * total + b * block, 8)
            put(wide, pl.ds(at, block), right(take(recv, pl.ds(start, block)), tx))
            return inner

        lax.fori_loop(0, 2, forward_x, 0)

        def plane(j, inner):
            lines_x = jnp.concatenate(
                [take(wide, pl.ds(j + at, size, stride=step)) for at, size, step in spans], axis=0
            )
            both = left(tz[0], tz[1], lines_x)
            half = both.shape[0] // 2
            spectrum = both[:half] + turned(both[half:], 1.0)
            factor = gain[c * group + j]
            spectrum = spectrum * jnp.concatenate([factor, factor], axis=1)
            both = left(tiz[0], tiz[1], spectrum)
            half = both.shape[0] // 2
            lines_z = both[:half] + turned(both[half:], -1.0)
            for k, (at, size, step) in enumerate(spans):
                put(wide, pl.ds(j + at, size, stride=step), lines_z[k * size : (k + 1) * size])
            return inner

        lax.fori_loop(0, group, plane, 0)

        def inverse_x(b, inner):
            at = pl.multiple_of(b * block, 8)
            start = pl.multiple_of(c * total + b * block, 8)
            put(back, pl.ds(start, block), right(take(wide, pl.ds(at, block)), tix))
            return inner

        lax.fori_loop(0, 2, inverse_x, 0)
        push(c, back, home, back_sem, home_sem)
        return carry

    lax.fori_loop(0, chunks, middle, 0)
    for c in range(chunks):
        left_sent(c, send, send_sem)

    def inverse_y(c, z):
        lines_y = jnp.concatenate(
            [take(home, pl.ds(c * total + z * group + j, n, stride=rows)) for j in range(group)], axis=0
        )
        both = left(tiy[0, c], tiy[1, c], lines_y)
        half = both.shape[0] // 2
        value = both[:half] + turned(both[half:], -1.0)
        if c:
            value = value + take(send, pl.ds(z * half, half))
        if c < chunks - 1:
            put(send, pl.ds(z * half, half), value)
        else:
            finish(z, value)

    def over(c):
        def plane(z, carry):
            inverse_y(c, z)
            return carry

        return plane

    for c in range(chunks):
        arrived(c, home, home_sem)
        if c < chunks - 1:
            lax.fori_loop(0, planes, over(c), 0)
    inverse(over(chunks - 1))
    for c in range(chunks):
        left_sent(c, back, back_sem)


def plan(shape, kernel, n):
    planes, width, double = shape
    own, grid_len, _ = kernel.shape
    fits = [g for g in range(1, own + 1) if own % g == 0 and g * planes % 8 == 0]
    group = fits[0] if fits else own
    chunks = own // group
    rows = -(-planes * group // 8) * 8
    total = n * rows
    tables = tables_of(grid_len, width, n, chunks, group, rows == planes * group)
    flat = pltpu.VMEM((double // LANES, chunks * total, LANES), f32)
    dma = pltpu.SemaphoreType.DMA
    tables[0] = tables[0].reshape(2, chunks, 2 * group * n, width)
    scratch = [
        flat, flat, flat, flat,
        pltpu.VMEM(kernel.shape, f32),
        pltpu.VMEM((2 * grid_len // LANES, total, LANES), f32),
        dma((chunks,)), dma((chunks,)), dma((chunks,)), dma((chunks,)), dma(()),
    ]
    return chunks, group, tables, scratch


def fused(image, prox_point, dual, adjoint, coil, kernel, n):
    _, planes, edge, width = image.shape
    chunks, group, tables, scratch = plan((planes, edge, 2 * width), kernel, n)
    haar = np.zeros((2, 2 * width, 2 * width), np.float32)
    for offset in range(2):
        for part in range(2):
            first = (np.arange(width // 2) * 2 + offset) % width + part * width
            second = (np.arange(width // 2) * 2 + offset + 1) % width + part * width
            haar[offset, first, first] = haar[offset, first, second] = 1.0
            haar[offset, second, first] = 1.0
            haar[offset, second, second] = -1.0
    tables.append(haar.astype(bf16))
    vmem = pl.BlockSpec(memory_space=pltpu.VMEM)
    apart = pl.BlockSpec(memory_space=pl.ANY)
    held = [pltpu.VMEM(image.shape, f32)] * 6
    held += [pltpu.VMEM(t.shape, bf16) for t in tables[1:]]
    lines = pltpu.VMEM((2 * width // LANES, (planes + 2) * edge, LANES), f32)
    dma = pltpu.SemaphoreType.DMA
    return pl.pallas_call(
        functools.partial(step_kernel, n, planes, chunks, group),
        out_shape=[jax.ShapeDtypeStruct(image.shape, f32)] * 3,
        in_specs=[vmem, vmem] + [apart] * 4 + [vmem] + [apart] * 6,
        out_specs=[apart] * 3,
        scratch_shapes=held + [lines, lines, dma((9,)), dma((2,)), dma((2,)), dma((7,))] + scratch,
        compiler_params=pltpu.CompilerParams(
            collective_id=0, has_side_effects=True, vmem_limit_bytes=67043328
        ),
        name="fused",
    )(image, coil, prox_point, dual, adjoint, kernel, *tables)


def filtered(field, kernel, n):
    planes = field.shape[0]
    chunks, group, tables, scratch = plan(field.shape, kernel, n)
    vmem = pl.BlockSpec(memory_space=pltpu.VMEM)
    return pl.pallas_call(
        functools.partial(filter_kernel, n, planes, chunks, group),
        out_shape=jax.ShapeDtypeStruct(field.shape, f32),
        in_specs=[vmem, pl.BlockSpec(memory_space=pl.ANY)] + [vmem] * 6,
        out_specs=vmem,
        scratch_shapes=scratch,
        compiler_params=pltpu.CompilerParams(
            collective_id=0, has_side_effects=True, vmem_limit_bytes=60 * 1024 * 1024
        ),
        name="filtered",
    )(field, kernel, *tables)


def pair(values, axis, first):
    length = values.shape[axis]
    after_one = pltpu.roll(values, length - 1, axis)
    before_one = pltpu.roll(values, 1, axis)
    return jnp.where(first, values + after_one, before_one - values)


def blocks(first, second, offset):
    shape = first[0].shape
    row_first = (lax.broadcasted_iota(jnp.int32, shape, 0) + offset) % 2 == 0
    col_first = (lax.broadcasted_iota(jnp.int32, shape, 1) + offset) % 2 == 0
    norm = half_root * half_root * half_root
    sums = [a + b for a, b in zip(first, second)]
    diffs = [a - b for a, b in zip(first, second)]
    result = []
    for which, parts in ((0, sums), (1, diffs)):
        coefs = [pair(pair(p, 0, row_first), 1, col_first) * norm for p in parts]
        magnitude = jnp.sqrt(coefs[0] * coefs[0] + coefs[1] * coefs[1])
        factor = jnp.maximum(magnitude - shrink, 0.0) / jnp.maximum(magnitude, shrink)
        if which == 0:
            factor = jnp.where(row_first & col_first, 1.0, factor)
        result.append(
            [pair(pair(p * factor, 1, col_first), 0, row_first) * norm for p in coefs]
        )
    low = [a + b for a, b in zip(*result)]
    high = [a - b for a, b in zip(*result)]
    return low, high


def spin_kernel(merged, below, above, image_new, dual, prox, dual_new):
    planes = merged.shape[1]

    def read(z):
        return [merged[0, z], merged[1, z]]

    def even(k, carry):
        low, high = blocks(read(2 * k), read(2 * k + 1), 0)
        for part in range(2):
            prox[part, 2 * k] = 0.5 * low[part]
            prox[part, 2 * k + 1] = 0.5 * high[part]
        return carry

    lax.fori_loop(0, planes // 2, even, 0)

    def finish(part, z, value):
        full = prox[part, z] + 0.5 * value
        prox[part, z] = full
        dual_new[part, z] = dual[part, z] + image_new[part, z] - full

    def odd(k, carry):
        low, high = blocks(read(2 * k + 1), read(2 * k + 2), 1)
        for part in range(2):
            finish(part, 2 * k + 1, low[part])
            finish(part, 2 * k + 2, high[part])
        return carry

    lax.fori_loop(0, planes // 2 - 1, odd, 0)
    _, high = blocks([below[0, 0], below[1, 0]], read(0), 1)
    low, _ = blocks(read(planes - 1), [above[0, 0], above[1, 0]], 1)
    for part in range(2):
        finish(part, 0, high[part])
        finish(part, planes - 1, low[part])


def pair_local(values, axis_dim, offset):
    length = values.shape[axis_dim]
    layout = [1] * values.ndim
    layout[axis_dim] = length
    is_first = ((jnp.arange(length) - offset) % 2 == 0).reshape(layout)
    after_one = jnp.roll(values, -1, axis_dim)
    before_one = jnp.roll(values, 1, axis_dim)
    return jnp.where(is_first, (values + after_one) * half_root, (before_one - values) * half_root)


def pair_planes(extended, own_first):
    middle = extended[:, 1:-1]
    after_one = extended[:, 2:]
    before_one = extended[:, :-2]
    marked = own_first[None, :, None, None]
    return jnp.where(marked, (middle + after_one) * half_root, (before_one - middle) * half_root)


def spin(extended, base, offset):
    total_planes = extended.shape[1]
    global_plane = base - 1 + jnp.arange(total_planes, dtype=jnp.int32)
    plane_first = (global_plane - offset) % 2 == 0
    own_first = plane_first[1:-1]
    lower_rim = (extended[:, :1] + extended[:, 1:2]) * half_root
    upper_rim = (extended[:, -2:-1] - extended[:, -1:]) * half_root
    coefs = jnp.concatenate([lower_rim, pair_planes(extended, own_first), upper_rim], axis=1)
    coefs = pair_local(coefs, 2, offset)
    coefs = pair_local(coefs, 3, offset)
    rows_first = (jnp.arange(extended.shape[2]) - offset) % 2 == 0
    cols_first = (jnp.arange(extended.shape[3]) - offset) % 2 == 0
    keep = plane_first[:, None, None] & rows_first[None, :, None] & cols_first[None, None, :]
    magnitude = jnp.sqrt(coefs[0] * coefs[0] + coefs[1] * coefs[1])
    factor = jnp.maximum(magnitude - shrink, 0.0) / jnp.maximum(magnitude, shrink)
    coefs = jnp.where(keep[None], coefs, coefs * factor[None])
    coefs = pair_local(coefs, 3, offset)
    coefs = pair_local(coefs, 2, offset)
    return pair_planes(coefs, own_first)


def on_device(n, coils, image, prox_point, dual, adjoint_data, coil_maps, kernel):
    width = image.shape[3]
    if coils == 1 and coil_maps.shape[0] == 1 and image.shape[1] % 2 == 0:
        return tuple(fused(image, prox_point, dual, adjoint_data, coil_maps[0], kernel, n))
    local_real = 0.0
    local_imag = 0.0
    for coil in range(coil_maps.shape[0]):
        sens_real = coil_maps[coil, 0]
        sens_imag = coil_maps[coil, 1]
        field = jnp.concatenate(
            [sens_real * image[0] - sens_imag * image[1], sens_real * image[1] + sens_imag * image[0]],
            axis=-1,
        )
        back = filtered(field, kernel, n)
        back_real, back_imag = back[..., :width], back[..., width:]
        local_real = local_real + (sens_real * back_real + sens_imag * back_imag)
        local_imag = local_imag + (sens_real * back_imag - sens_imag * back_real)
    normal_real, normal_imag = lax.psum((local_real, local_imag), "coil")
    normal = jnp.stack([normal_real, normal_imag])
    image_new = image - step_size * (normal - adjoint_data + penalty * (image - prox_point + dual))
    merged = image_new + dual
    planes = merged.shape[1]
    below = lax.ppermute(merged[:, -1:], "slab", [(i, (i + 1) % n) for i in range(n)])
    above = lax.ppermute(merged[:, :1], "slab", [((i + 1) % n, i) for i in range(n)])
    if planes % 2:
        extended = jnp.concatenate([below, merged, above], axis=1)
        base = lax.axis_index("slab") * planes
        prox_new = 0.5 * (spin(extended, base, 0) + spin(extended, base, 1))
        return (image_new, prox_new, dual + image_new - prox_new)
    vmem = pl.BlockSpec(memory_space=pltpu.VMEM)
    prox_new, dual_new = pl.pallas_call(
        spin_kernel,
        out_shape=[jax.ShapeDtypeStruct(image.shape, f32)] * 2,
        in_specs=[vmem] * 5,
        out_specs=[vmem] * 2,
        compiler_params=pltpu.CompilerParams(vmem_limit_bytes=48 * 1024 * 1024),
        name="spin",
    )(merged, below, above, image_new, dual)
    return (image_new, prox_new, dual_new)


def solution(mesh):
    n = mesh.shape["slab"]
    field = P("recon", "slab", None, None)
    return jax.shard_map(
        functools.partial(on_device, n, mesh.shape["coil"]),
        mesh=mesh,
        in_specs=(field, field, field, field, P("coil", "recon", "slab", None, None), P("slab", None, None)),
        out_specs=(field, field, field),
        check_vma=False,
    )
```

```python
import functools
import math

import jax
import jax.numpy as jnp
import numpy as np
from jax import lax
from jax.experimental import pallas as pl
from jax.experimental.pallas import tpu as pltpu
from jax.sharding import PartitionSpec as P

half_root = 0.7071067811865476
shrink = 0.5
step_size = 0.25
penalty = 1.0
MESH = pl.DeviceIdType.MESH
f32 = jnp.float32
bf16 = jnp.bfloat16
LANES = 128


def halves(table):
    table = table.astype(np.float32)
    hi = table.astype(bf16)
    lo = (table - hi.astype(np.float32)).astype(bf16)
    return np.stack([hi, lo])


def tables_of(grid_len, width, n, chunks, group, dense):
    cells = np.arange(width)
    freqs = np.arange(grid_len)
    angle = 2.0 * math.pi / grid_len * (np.outer(cells, freqs) % grid_len)
    cos, sin = np.cos(angle), np.sin(angle)
    table_x = np.block([[cos, -sin], [sin, cos]])
    table_z = np.concatenate([cos.T, sin.T])
    table_iz = np.concatenate([cos, sin]) / grid_len
    if not dense:
        by_plane = np.arange(width).reshape(n, -1).T.reshape(-1)
        table_z = table_z[:, by_plane]
        table_iz = np.concatenate([cos[by_plane], sin[by_plane]]) / grid_len
    table_ix = np.block([[cos.T, sin.T], [-sin.T, cos.T]]) / grid_len
    own = chunks * group
    c, j, d = np.meshgrid(np.arange(chunks), np.arange(group), np.arange(n), indexing="ij")
    order = (d * own + c * group + j).reshape(chunks, group * n)
    table_y = np.concatenate([cos.T[order], sin.T[order]], axis=1)
    c, j, s = np.meshgrid(np.arange(chunks), np.arange(group), np.arange(n), indexing="ij")
    order = (s * own + c * group + j).reshape(chunks, 1, -1)
    both = np.concatenate([cos, sin])[:, :] / grid_len
    table_iy = np.stack([both[:, order[c, 0]] for c in range(chunks)])
    return [halves(t) for t in (table_y, table_x, table_z, table_iz, table_ix, table_iy)]


def split(values):
    hi = values.astype(bf16)
    return hi, (values - hi.astype(f32)).astype(bf16)


def mm(a, b):
    return jnp.dot(a, b, preferred_element_type=f32)


def right(values, table):
    hi, lo = split(values)
    return mm(hi, table[0]) + mm(lo, table[0]) + mm(hi, table[1])


def left(table_hi, table_lo, values):
    hi, lo = split(values)
    return mm(table_hi, hi) + mm(table_hi, lo) + mm(table_lo, hi)


def turned(values, sign):
    half = values.shape[-1] // 2
    low, high = values[:, :half], values[:, half:]
    return jnp.concatenate([high * sign, low * -sign], axis=1)


def take(ref, rows):
    return jnp.concatenate([ref[l, rows, :] for l in range(ref.shape[0])], axis=1)


def put(ref, rows, values):
    for l in range(ref.shape[0]):
        ref[l, rows, :] = values[:, l * LANES : (l + 1) * LANES]


def filter_kernel(n, planes, chunks, group, field, gain_in, ty, tx, tz, tiz, tix, tiy, out, *scratch):
    def finish(z, value):
        out[z] = value

    def inverse(plane):
        lax.fori_loop(0, planes, plane, 0)

    filter_body(
        n, planes, chunks, group, lambda z: field[z], finish, (lambda: None, lambda: None), inverse,
        gain_in, ty, tx, tz, tiz, tix, tiy, *scratch,
    )


def spin_pair(mg, px, table, edge, first, second, offset, add):
    count = edge // 2

    def rows(plane, odd):
        return pl.ds(plane * edge + odd, count, stride=2)

    def lines(plane):
        even, odd = take(mg, rows(plane, 0)), take(mg, rows(plane, 1))
        return (odd, pltpu.roll(even, count - 1, 0)) if offset else (even, odd)

    (f0, s0), (f1, s1) = lines(first), lines(second)
    uf, us, vf, vs = f0 + f1, s0 + s1, f0 - f1, s0 - s1
    cells = jnp.concatenate([uf + us, uf - us, vf + vs, vf - vs], axis=0)

    def along_x(values):
        hi, lo = split(values)
        return mm(hi, table[offset]) + mm(lo, table[offset])

    coefs = along_x(cells)
    squares = coefs * coefs
    half = squares.shape[1] // 2
    squares = squares + jnp.concatenate([squares[:, half:], squares[:, :half]], axis=1)
    factor = 1.0 - lax.rsqrt(jnp.maximum(0.5 * squares, 1.0))
    row = lax.broadcasted_iota(jnp.int32, factor.shape, 0)
    col = lax.broadcasted_iota(jnp.int32, factor.shape, 1)
    factor = jnp.where((row < count) & ((col + offset) % 2 == 0), 1.0, factor)
    cells = along_x(coefs * factor) * 0.0625
    uf, us, vf, vs = (cells[k * count : (k + 1) * count] for k in range(4))
    uf, us, vf, vs = uf + us, uf - us, vf + vs, vf - vs
    for plane, f, s in ((first, uf + vf, us + vs), (second, uf - vf, us - vs)):
        even, odd = (pltpu.roll(s, 1, 0), f) if offset else (f, s)
        if add:
            even = even + take(px, rows(plane, 0))
            odd = odd + take(px, rows(plane, 1))
        put(px, rows(plane, 0), even)
        put(px, rows(plane, 1), odd)


def step_kernel(
    n, planes, chunks, group,
    image, coil, late_a, late_b, late_c, gain_in, ty,
    ltx, ltz, ltiz, ltix, ltiy, lpx,
    image_out, prox_out, dual_out,
    image_new, prox_new, dual_new, prox_point, dual, adjoint, tx, tz, tiz, tix, tiy, table, mg, px,
    late_sem, halo_out, halo_in, out_sem, *scratch,
):
    me = lax.axis_index("slab")
    edge, width = image.shape[2:]
    pairs = [
        (ltx, tx), (ltz, tz), (ltiz, tiz), (ltix, tix), (ltiy, tiy), (lpx, table),
        (late_a, prox_point), (late_b, dual), (late_c, adjoint),
    ]
    copies = [pltpu.make_async_copy(a, b, late_sem.at[k]) for k, (a, b) in enumerate(pairs)]

    def begin():
        for copy in copies:
            copy.start()

    def ready():
        for copy in copies:
            copy.wait()

    def field(z):
        sr, si, re, im = coil[0, z], coil[1, z], image[0, z], image[1, z]
        return jnp.concatenate([sr * re - si * im, sr * im + si * re], axis=1)

    def finish(z, value):
        back = (value[:, :width], value[:, width:])
        sr, si = coil[0, z], coil[1, z]
        normal = (sr * back[0] + si * back[1], sr * back[1] - si * back[0])
        merged = []
        for part in range(2):
            old, point, scaled = image[part, z], prox_point[part, z], dual[part, z]
            new = old - step_size * (normal[part] - adjoint[part, z] + penalty * (old - point + scaled))
            image_new[part, z] = new
            merged.append(new + scaled)
        put(mg, pl.ds((z + 1) * edge, edge), jnp.concatenate(merged, axis=1))

    def span(plane):
        return mg.at[:, pl.ds(plane * edge, edge)]

    up = pltpu.make_async_remote_copy(
        src_ref=span(planes), dst_ref=span(0), send_sem=halo_out.at[0], recv_sem=halo_in.at[0],
        device_id={"slab": lax.rem(me + 1, n)}, device_id_type=MESH,
    )
    down = pltpu.make_async_remote_copy(
        src_ref=span(1), dst_ref=span(planes + 1), send_sem=halo_out.at[1], recv_sem=halo_in.at[1],
        device_id={"slab": lax.rem(me + n - 1, n)}, device_id_type=MESH,
    )

    def inverse(plane):
        def rim(k, carry):
            return plane(k * (planes - 1), carry)

        lax.fori_loop(0, 2, rim, 0)
        up.start()
        down.start()
        lax.fori_loop(1, planes - 1, plane, 0)

    filter_body(
        n, planes, chunks, group, field, finish, (begin, ready), inverse,
        gain_in, ty, tx, tz, tiz, tix, tiy, *scratch,
    )

    written = [pltpu.make_async_copy(image_new, image_out, out_sem.at[0])]
    written[0].start()

    def write(k, start, size):
        for buffer, whole in ((prox_new, prox_out), (dual_new, dual_out)):
            part = pl.ds(start, size)
            copy = pltpu.make_async_copy(buffer.at[:, part], whole.at[:, part], out_sem.at[k])
            copy.start()
            written.append(copy)
            k += 1

    for plane in (0, planes + 1):
        put(px, pl.ds(plane * edge, edge), jnp.zeros((edge, 2 * width), f32))

    def even(k, carry):
        spin_pair(mg, px, table, edge, 2 * k + 1, 2 * k + 2, 0, False)
        return carry

    def odd(k, carry):
        spin_pair(mg, px, table, edge, 2 * k, 2 * k + 1, 1, True)
        return carry

    def rim(k, carry):
        return odd(k * (planes // 2), carry)

    def close(z, carry):
        at = pl.ds((z + 1) * edge, edge)
        prox = take(px, at)
        scaled = take(mg, at) - prox
        for part in range(2):
            prox_new[part, z] = prox[:, part * width : (part + 1) * width]
            dual_new[part, z] = scaled[:, part * width : (part + 1) * width]
        return carry

    lax.fori_loop(0, planes // 2, even, 0)
    lax.fori_loop(1, planes // 2, odd, 0)
    if planes > 2:
        lax.fori_loop(1, planes - 1, close, 0)
        write(1, 1, planes - 2)
    up.wait()
    down.wait()
    lax.fori_loop(0, 2, rim, 0)
    lax.fori_loop(0, 2, lambda k, carry: close(k * (planes - 1), carry), 0)
    write(3, 0, 1)
    write(5, planes - 1, 1)
    for copy in written:
        copy.wait()


def filter_body(
    n, planes, chunks, group, field, finish, late, inverse,
    gain_in, ty, tx, tz, tiz, tix, tiy,
    send, recv, back, home, gain, wide,
    send_sem, recv_sem, back_sem, home_sem, gain_sem,
):
    begin, ready = late
    me = lax.axis_index("slab")
    rows = send.shape[1] // (n * chunks)
    total = n * rows
    if rows == planes * group:
        spans = [(0, n * planes, group)]
    else:
        spans = [(z * group, n, rows) for z in range(planes)]

    gain_copy = pltpu.make_async_copy(gain_in, gain, gain_sem)
    gain_copy.start()
    barrier = pltpu.get_barrier_semaphore()

    def greet(i, carry):
        pl.semaphore_signal(
            barrier, inc=1, device_id={"slab": lax.rem(me + i, n)}, device_id_type=MESH
        )
        return carry

    lax.fori_loop(1, n, greet, 0)
    begin()

    def push(c, source, target, s_sem, r_sem):
        def one(i, carry):
            far = n // 2 + (i // 2) * (2 * (i % 2) - 1)
            to = lax.rem(me + far, n)
            pltpu.make_async_remote_copy(
                src_ref=source.at[:, pl.ds(pl.multiple_of(c * total + to * rows, 8), rows)],
                dst_ref=target.at[:, pl.ds(pl.multiple_of(c * total + me * rows, 8), rows)],
                send_sem=s_sem.at[c],
                recv_sem=r_sem.at[c],
                device_id={"slab": to},
                device_id_type=MESH,
            ).start()
            return carry

        lax.fori_loop(1, n, one, 0)
        own = pl.ds(pl.multiple_of(c * total + me * rows, 8), rows)
        pltpu.make_async_copy(source.at[:, own], target.at[:, own], r_sem.at[c]).start()

    def arrived(c, target, r_sem):
        span = target.at[:, pl.ds(pl.multiple_of(c * total, 8), total)]
        pltpu.make_async_copy(span, span, r_sem.at[c]).wait()

    def left_sent(c, source, s_sem):
        span = source.at[:, pl.ds(pl.multiple_of(c * total, 8), total - rows)]
        pltpu.make_async_copy(span, span, s_sem.at[c]).wait()

    def forward_y(c):
        def plane(z, carry):
            both = left(ty[0, c], ty[1, c], field(z))
            half = group * n
            lines_y = both[:half] + turned(both[half:], 1.0)
            for j in range(group):
                at = pl.ds(c * total + z * group + j, n, stride=rows)
                put(send, at, lines_y[j * n : (j + 1) * n])
            return carry

        lax.fori_loop(0, planes, plane, 0)

    for c in range(chunks):
        forward_y(c)
        if c == 0:
            pl.semaphore_wait(barrier, n - 1)
        push(c, send, recv, send_sem, recv_sem)

    gain_copy.wait()
    ready()

    def flip(k, carry):
        gain[k] = jnp.transpose(gain[k])
        return carry

    lax.fori_loop(0, chunks * group, flip, 0)

    block = total // 2

    def middle(c, carry):
        arrived(c, recv, recv_sem)

        def forward_x(b, inner):
            at = pl.multiple_of(b * block, 8)
            start = pl.multiple_of(c * total + b * block, 8)
            put(wide, pl.ds(at, block), right(take(recv, pl.ds(start, block)), tx))
            return inner

        lax.fori_loop(0, 2, forward_x, 0)

        def plane(j, inner):
            lines_x = jnp.concatenate(
                [take(wide, pl.ds(j + at, size, stride=step)) for at, size, step in spans], axis=0
            )
            both = left(tz[0], tz[1], lines_x)
            half = both.shape[0] // 2
            spectrum = both[:half] + turned(both[half:], 1.0)
            factor = gain[c * group + j]
            spectrum = spectrum * jnp.concatenate([factor, factor], axis=1)
            both = left(tiz[0], tiz[1], spectrum)
            half = both.shape[0] // 2
            lines_z = both[:half] + turned(both[half:], -1.0)
            for k, (at, size, step) in enumerate(spans):
                put(wide, pl.ds(j + at, size, stride=step), lines_z[k * size : (k + 1) * size])
            return inner

        lax.fori_loop(0, group, plane, 0)

        def inverse_x(b, inner):
            at = pl.multiple_of(b * block, 8)
            start = pl.multiple_of(c * total + b * block, 8)
            put(back, pl.ds(start, block), right(take(wide, pl.ds(at, block)), tix))
            return inner

        lax.fori_loop(0, 2, inverse_x, 0)
        push(c, back, home, back_sem, home_sem)
        return carry

    lax.fori_loop(0, chunks, middle, 0)
    for c in range(chunks):
        left_sent(c, send, send_sem)

    def inverse_y(c, z):
        lines_y = jnp.concatenate(
            [take(home, pl.ds(c * total + z * group + j, n, stride=rows)) for j in range(group)], axis=0
        )
        both = left(tiy[0, c], tiy[1, c], lines_y)
        half = both.shape[0] // 2
        value = both[:half] + turned(both[half:], -1.0)
        if c:
            value = value + take(send, pl.ds(z * half, half))
        if c < chunks - 1:
            put(send, pl.ds(z * half, half), value)
        else:
            finish(z, value)

    def over(c):
        def plane(z, carry):
            inverse_y(c, z)
            return carry

        return plane

    for c in range(chunks):
        arrived(c, home, home_sem)
        if c < chunks - 1:
            lax.fori_loop(0, planes, over(c), 0)
    inverse(over(chunks - 1))
    for c in range(chunks):
        left_sent(c, back, back_sem)


def plan(shape, kernel, n):
    planes, width, double = shape
    own, grid_len, _ = kernel.shape
    fits = [g for g in range(1, own + 1) if own % g == 0 and g * planes % 8 == 0]
    group = fits[0] if fits else own
    chunks = own // group
    rows = -(-planes * group // 8) * 8
    total = n * rows
    tables = tables_of(grid_len, width, n, chunks, group, rows == planes * group)
    flat = pltpu.VMEM((double // LANES, chunks * total, LANES), f32)
    dma = pltpu.SemaphoreType.DMA
    tables[0] = tables[0].reshape(2, chunks, 2 * group * n, width)
    scratch = [
        flat, flat, flat, flat,
        pltpu.VMEM(kernel.shape, f32),
        pltpu.VMEM((2 * grid_len // LANES, total, LANES), f32),
        dma((chunks,)), dma((chunks,)), dma((chunks,)), dma((chunks,)), dma(()),
    ]
    return chunks, group, tables, scratch


def fused(image, prox_point, dual, adjoint, coil, kernel, n):
    _, planes, edge, width = image.shape
    chunks, group, tables, scratch = plan((planes, edge, 2 * width), kernel, n)
    haar = np.zeros((2, 2 * width, 2 * width), np.float32)
    for offset in range(2):
        for part in range(2):
            first = (np.arange(width // 2) * 2 + offset) % width + part * width
            second = (np.arange(width // 2) * 2 + offset + 1) % width + part * width
            haar[offset, first, first] = haar[offset, first, second] = 1.0
            haar[offset, second, first] = 1.0
            haar[offset, second, second] = -1.0
    tables.append(haar.astype(bf16))
    vmem = pl.BlockSpec(memory_space=pltpu.VMEM)
    apart = pl.BlockSpec(memory_space=pl.ANY)
    held = [pltpu.VMEM(image.shape, f32)] * 6
    held += [pltpu.VMEM(t.shape, bf16) for t in tables[1:]]
    lines = pltpu.VMEM((2 * width // LANES, (planes + 2) * edge, LANES), f32)
    dma = pltpu.SemaphoreType.DMA
    return pl.pallas_call(
        functools.partial(step_kernel, n, planes, chunks, group),
        out_shape=[jax.ShapeDtypeStruct(image.shape, f32)] * 3,
        in_specs=[vmem, vmem] + [apart] * 4 + [vmem] + [apart] * 6,
        out_specs=[apart] * 3,
        scratch_shapes=held + [lines, lines, dma((9,)), dma((2,)), dma((2,)), dma((7,))] + scratch,
        compiler_params=pltpu.CompilerParams(
            collective_id=0, has_side_effects=True, vmem_limit_bytes=67043328
        ),
        name="fused",
    )(image, coil, prox_point, dual, adjoint, kernel, *tables)


def filtered(field, kernel, n):
    planes = field.shape[0]
    chunks, group, tables, scratch = plan(field.shape, kernel, n)
    vmem = pl.BlockSpec(memory_space=pltpu.VMEM)
    return pl.pallas_call(
        functools.partial(filter_kernel, n, planes, chunks, group),
        out_shape=jax.ShapeDtypeStruct(field.shape, f32),
        in_specs=[vmem, pl.BlockSpec(memory_space=pl.ANY)] + [vmem] * 6,
        out_specs=vmem,
        scratch_shapes=scratch,
        compiler_params=pltpu.CompilerParams(
            collective_id=0, has_side_effects=True, vmem_limit_bytes=60 * 1024 * 1024
        ),
        name="filtered",
    )(field, kernel, *tables)


def pair(values, axis, first):
    length = values.shape[axis]
    after_one = pltpu.roll(values, length - 1, axis)
    before_one = pltpu.roll(values, 1, axis)
    return jnp.where(first, values + after_one, before_one - values)


def blocks(first, second, offset):
    shape = first[0].shape
    row_first = (lax.broadcasted_iota(jnp.int32, shape, 0) + offset) % 2 == 0
    col_first = (lax.broadcasted_iota(jnp.int32, shape, 1) + offset) % 2 == 0
    norm = half_root * half_root * half_root
    sums = [a + b for a, b in zip(first, second)]
    diffs = [a - b for a, b in zip(first, second)]
    result = []
    for which, parts in ((0, sums), (1, diffs)):
        coefs = [pair(pair(p, 0, row_first), 1, col_first) * norm for p in parts]
        magnitude = jnp.sqrt(coefs[0] * coefs[0] + coefs[1] * coefs[1])
        factor = jnp.maximum(magnitude - shrink, 0.0) / jnp.maximum(magnitude, shrink)
        if which == 0:
            factor = jnp.where(row_first & col_first, 1.0, factor)
        result.append(
            [pair(pair(p * factor, 1, col_first), 0, row_first) * norm for p in coefs]
        )
    low = [a + b for a, b in zip(*result)]
    high = [a - b for a, b in zip(*result)]
    return low, high


def spin_kernel(merged, below, above, image_new, dual, prox, dual_new):
    planes = merged.shape[1]

    def read(z):
        return [merged[0, z], merged[1, z]]

    def even(k, carry):
        low, high = blocks(read(2 * k), read(2 * k + 1), 0)
        for part in range(2):
            prox[part, 2 * k] = 0.5 * low[part]
            prox[part, 2 * k + 1] = 0.5 * high[part]
        return carry

    lax.fori_loop(0, planes // 2, even, 0)

    def finish(part, z, value):
        full = prox[part, z] + 0.5 * value
        prox[part, z] = full
        dual_new[part, z] = dual[part, z] + image_new[part, z] - full

    def odd(k, carry):
        low, high = blocks(read(2 * k + 1), read(2 * k + 2), 1)
        for part in range(2):
            finish(part, 2 * k + 1, low[part])
            finish(part, 2 * k + 2, high[part])
        return carry

    lax.fori_loop(0, planes // 2 - 1, odd, 0)
    _, high = blocks([below[0, 0], below[1, 0]], read(0), 1)
    low, _ = blocks(read(planes - 1), [above[0, 0], above[1, 0]], 1)
    for part in range(2):
        finish(part, 0, high[part])
        finish(part, planes - 1, low[part])


def pair_local(values, axis_dim, offset):
    length = values.shape[axis_dim]
    layout = [1] * values.ndim
    layout[axis_dim] = length
    is_first = ((jnp.arange(length) - offset) % 2 == 0).reshape(layout)
    after_one = jnp.roll(values, -1, axis_dim)
    before_one = jnp.roll(values, 1, axis_dim)
    return jnp.where(is_first, (values + after_one) * half_root, (before_one - values) * half_root)


def pair_planes(extended, own_first):
    middle = extended[:, 1:-1]
    after_one = extended[:, 2:]
    before_one = extended[:, :-2]
    marked = own_first[None, :, None, None]
    return jnp.where(marked, (middle + after_one) * half_root, (before_one - middle) * half_root)


def spin(extended, base, offset):
    total_planes = extended.shape[1]
    global_plane = base - 1 + jnp.arange(total_planes, dtype=jnp.int32)
    plane_first = (global_plane - offset) % 2 == 0
    own_first = plane_first[1:-1]
    lower_rim = (extended[:, :1] + extended[:, 1:2]) * half_root
    upper_rim = (extended[:, -2:-1] - extended[:, -1:]) * half_root
    coefs = jnp.concatenate([lower_rim, pair_planes(extended, own_first), upper_rim], axis=1)
    coefs = pair_local(coefs, 2, offset)
    coefs = pair_local(coefs, 3, offset)
    rows_first = (jnp.arange(extended.shape[2]) - offset) % 2 == 0
    cols_first = (jnp.arange(extended.shape[3]) - offset) % 2 == 0
    keep = plane_first[:, None, None] & rows_first[None, :, None] & cols_first[None, None, :]
    magnitude = jnp.sqrt(coefs[0] * coefs[0] + coefs[1] * coefs[1])
    factor = jnp.maximum(magnitude - shrink, 0.0) / jnp.maximum(magnitude, shrink)
    coefs = jnp.where(keep[None], coefs, coefs * factor[None])
    coefs = pair_local(coefs, 3, offset)
    coefs = pair_local(coefs, 2, offset)
    return pair_planes(coefs, own_first)


def on_device(n, coils, image, prox_point, dual, adjoint_data, coil_maps, kernel):
    width = image.shape[3]
    if coils == 1 and coil_maps.shape[0] == 1 and image.shape[1] % 2 == 0:
        return tuple(fused(image, prox_point, dual, adjoint_data, coil_maps[0], kernel, n))
    local_real = 0.0
    local_imag = 0.0
    for coil in range(coil_maps.shape[0]):
        sens_real = coil_maps[coil, 0]
        sens_imag = coil_maps[coil, 1]
        field = jnp.concatenate(
            [sens_real * image[0] - sens_imag * image[1], sens_real * image[1] + sens_imag * image[0]],
            axis=-1,
        )
        back = filtered(field, kernel, n)
        back_real, back_imag = back[..., :width], back[..., width:]
        local_real = local_real + (sens_real * back_real + sens_imag * back_imag)
        local_imag = local_imag + (sens_real * back_imag - sens_imag * back_real)
    normal_real, normal_imag = lax.psum((local_real, local_imag), "coil")
    normal = jnp.stack([normal_real, normal_imag])
    image_new = image - step_size * (normal - adjoint_data + penalty * (image - prox_point + dual))
    merged = image_new + dual
    planes = merged.shape[1]
    below = lax.ppermute(merged[:, -1:], "slab", [(i, (i + 1) % n) for i in range(n)])
    above = lax.ppermute(merged[:, :1], "slab", [((i + 1) % n, i) for i in range(n)])
    if planes % 2:
        extended = jnp.concatenate([below, merged, above], axis=1)
        base = lax.axis_index("slab") * planes
        prox_new = 0.5 * (spin(extended, base, 0) + spin(extended, base, 1))
        return (image_new, prox_new, dual + image_new - prox_new)
    vmem = pl.BlockSpec(memory_space=pltpu.VMEM)
    prox_new, dual_new = pl.pallas_call(
        spin_kernel,
        out_shape=[jax.ShapeDtypeStruct(image.shape, f32)] * 2,
        in_specs=[vmem] * 5,
        out_specs=[vmem] * 2,
        compiler_params=pltpu.CompilerParams(vmem_limit_bytes=48 * 1024 * 1024),
        name="spin",
    )(merged, below, above, image_new, dual)
    return (image_new, prox_new, dual_new)


def solution(mesh):
    n = mesh.shape["slab"]
    field = P("recon", "slab", None, None)
    return jax.shard_map(
        functools.partial(on_device, n, mesh.shape["coil"]),
        mesh=mesh,
        in_specs=(field, field, field, field, P("coil", "recon", "slab", None, None), P("slab", None, None)),
        out_specs=(field, field, field),
        check_vma=False,
    )
```
